256 devices in a mesh: row: 16 (over y, x), col: 16 (over z, core).
Axes of the slice: x: 4, y: 4, z: 8, core: 2. Of those that a mesh axis runs over, the one named last changes fastest.
Arguments:
- fitting: bfloat16 [512, 512, 256], P(('row', 'col')), may hold values from -6 to 6
- coefficients: bfloat16 [64, 64, 6, 256, 128], P('row', 'col'), may hold values from -0.375 to 0.375
- amplitudes: bfloat16 [64, 64, 4096], P('row', 'col'), may hold values from -6 to 6
- intersections: bfloat16 [64, 64, 8, 4096], P('row', 'col'), may hold values from -0.33 to 1.33
- virtual_energy: float32 [64, 64, 64], P('row', 'col'), may hold values from 0.2 to 2
- occupied_energy: float32 [64], replicated, may hold values from -1.5 to -0.3
- kept_count: int32 [64, 64], P('row', 'col'), may hold values from 16 to 64
- orbital_atoms: int32 [64, 3], replicated, may hold values from 0 to 511, as said below
- fock_partner: int32 [64, 4], replicated, may hold values from 0 to 63, as said below
- fock_value: float32 [64, 4], replicated, may hold values from -3 to 3
Outputs:
- residual: float32 [64, 64, 4096], P('row', 'col')
The draws below stay inside these ranges and needn't reach their ends.
Inputs may be any that keep to these rules, and one draw needn't show every extreme that they name: `orbital_atoms`: the 3 atoms of orbital i are different and lie in [(i // 4) * 32, (i // 4 + 1) * 32). fock_partner[i, n] differs from i by at most 4.
All inputs are finite; a program needn't handle non-finite values.
Results may differ from the reference program's by a relative error of at most 0.0029.
Values may be sent and summed in bfloat16 or wider, within the bound.
A program may use at most 128 MiB of HBM per device.

```python
import math
import jax
import jax.numpy as jnp
from jax import lax

AUX = 512
PAO = 256
NPNO = 64
DOMAIN = 3
PARTNERS = 4
I_DEV = 4
NOCC = 64
J_DEV = 4
NATOMS = 512
ROW_ATOMS = 32


def draw_intersections(key, part):
    first, second = jax.random.split(key)
    diagonal = jax.random.uniform(first, (NOCC, NOCC, 2 * PARTNERS, NPNO), jnp.float32, 0.7, 1.0)
    noise = jnp.clip(jax.random.normal(second, (NOCC, NOCC, 2 * PARTNERS, NPNO, NPNO), jnp.float32), -4.0, 4.0) * 0.08
    identity = jnp.eye(NPNO, dtype=jnp.float32)
    whole = noise + diagonal[..., :, None] * identity
    return whole.reshape(NOCC, NOCC, 2 * PARTNERS, NPNO * NPNO).astype(jnp.bfloat16)


def draw_orbital_atoms(key, part):
    scores = jax.random.randint(key, (NOCC, ROW_ATOMS), 0, 1 << 20) * ROW_ATOMS + jnp.arange(ROW_ATOMS, dtype=jnp.int32)[None, :]
    chosen = jnp.argsort(scores, axis=1, stable=True)[:, :DOMAIN].astype(jnp.int32)
    base = jnp.arange(NOCC, dtype=jnp.int32) // I_DEV * ROW_ATOMS
    return (chosen + base[:, None]).astype(jnp.int32)


def draw_fock_partner(key, part):
    first, second = jax.random.split(key)
    reach = jax.random.randint(first, (NOCC, PARTNERS), 1, J_DEV + 1)
    direction = 2 * jax.random.randint(second, (NOCC, PARTNERS), 0, 2) - 1
    target = jnp.arange(NOCC, dtype=jnp.int32)[:, None] + reach * direction
    target = jnp.where(target < 0, -target, target)
    target = jnp.where(target > NOCC - 1, 2 * (NOCC - 1) - target, target)
    return target.astype(jnp.int32)


def plant(entries, key, smallest, top_value):
    longest = entries.shape.index(max(entries.shape))
    spots = []
    for shift in (0, 1):
        where = [jax.random.randint(jax.random.fold_in(key, axis), (), 0, length) for axis, length in enumerate(entries.shape)]
        where[longest] = (where[longest] + shift) % entries.shape[longest]
        spots.append(tuple(where))
    return entries.at[spots[0]].set(smallest).at[spots[1]].set(top_value)


def block_levels(rng, dims, cuts, low, top_value):
    gain, own = 1.0, jax.random.fold_in(rng, 6)
    for dim, blocks in cuts:
        draws = jnp.exp(jax.random.uniform(jax.random.fold_in(own, dim), (blocks,), jnp.float32, low / len(cuts), top_value / len(cuts)))
        gain = gain * jnp.repeat(draws, dims[dim] // blocks).reshape([-1 if axis == dim else 1 for axis in range(len(dims))])
    return gain


def scatter_about(stream_key, dims, width, bound, cuts=(), kind=jnp.bfloat16):
    factor_of = block_levels(stream_key, dims, cuts, -0.22, 0.18) if cuts else 1.0
    entries = jax.random.normal(stream_key, dims, jnp.float32) * width * factor_of
    return jnp.minimum(jnp.maximum(entries, -bound), bound).astype(kind)


def setup_inputs(seed: int = 0) -> dict:
    key_of = jax.random.split(jax.random.key(seed), 11)
    fitting = scatter_about(key_of[0], (NATOMS, AUX, PAO), 1.0, 6.0, ((0, 256),))
    coefficients = scatter_about(key_of[1], (NOCC, NOCC, 2 * DOMAIN, PAO, 2 * NPNO), PAO ** -0.5, 0.375, ((0, 16), (1, 16)))
    amplitudes = scatter_about(key_of[2], (NOCC, NOCC, NPNO * NPNO), 1.0, 6.0, ((0, 16), (1, 16)))
    intersections = draw_intersections(jax.random.fold_in(key_of[10], 71), 0)
    virtual_energy = jnp.clip(jnp.exp(math.log(2.0) - 2.3025851 * jax.random.uniform(key_of[4], (NOCC, NOCC, NPNO), jnp.float32) ** block_levels(key_of[4], (NOCC, NOCC, NPNO), ((0, 16), (1, 16)), -0.2, 0.2)), 0.2, 2.0)
    occupied_energy = jnp.clip(jax.random.uniform(key_of[5], (NOCC,), jnp.float32, -1.5, -0.3), -1.5, -0.3)
    kept_count = plant(jax.random.randint(key_of[6], (NOCC, NOCC), NPNO // 4, NPNO + 1), jax.random.fold_in(key_of[6], 1), NPNO // 4, NPNO).astype(jnp.int32)
    orbital_atoms = draw_orbital_atoms(jax.random.fold_in(key_of[10], 71), 0)
    fock_partner = draw_fock_partner(jax.random.fold_in(key_of[10], 71), 0)
    fock_value = scatter_about(key_of[9], (NOCC, PARTNERS), 0.5, 3.0, (), jnp.float32)
    return dict(fitting=fitting, coefficients=coefficients, amplitudes=amplitudes, intersections=intersections, virtual_energy=virtual_energy, occupied_energy=occupied_energy, kept_count=kept_count, orbital_atoms=orbital_atoms, fock_partner=fock_partner, fock_value=fock_value)


def reference(fitting, coefficients, amplitudes, intersections, virtual_energy, occupied_energy, kept_count, orbital_atoms, fock_partner, fock_value):
    highest = lax.Precision.HIGHEST
    total = amplitudes.shape[0]
    matrices = amplitudes.reshape(total, total, NPNO, NPNO)
    column_fit = fitting[orbital_atoms].astype(jnp.float32)
    levels = jnp.arange(NPNO, dtype=jnp.int32)

    def one_row(orbital):
        row_fit = fitting[orbital_atoms[orbital]].astype(jnp.float32)
        mapping = coefficients[orbital].astype(jnp.float32)
        own_side = jnp.einsum("sap,jspq->jsaq", row_fit, mapping[:, :DOMAIN], precision=highest).astype(jnp.bfloat16).astype(jnp.float32)
        other_side = jnp.einsum("jsap,jspq->jsaq", column_fit, mapping[:, DOMAIN:], precision=highest).astype(jnp.bfloat16).astype(jnp.float32)
        exchange_part = jnp.einsum("jsaq,jsar->jqr", own_side[..., :NPNO], own_side[..., NPNO:], precision=highest)
        exchange_part = exchange_part + jnp.einsum("jsaq,jsar->jqr", other_side[..., :NPNO], other_side[..., NPNO:], precision=highest)
        exchange_part = exchange_part * ((2 * DOMAIN * AUX) ** -0.5)
        from_rows = jnp.transpose(matrices[fock_partner[orbital]], (1, 0, 2, 3))
        from_columns = matrices[orbital][fock_partner]
        partners = jnp.concatenate([from_rows, from_columns], axis=1).astype(jnp.float32)
        intersection_mats = intersections[orbital].reshape(total, 2 * PARTNERS, NPNO, NPNO).astype(jnp.float32)
        half = jnp.einsum("jnab,jnbc->jnac", intersection_mats, partners, precision=highest).astype(jnp.bfloat16)
        sandwich = jnp.einsum("jnac,jndc->jnad", half.astype(jnp.float32), intersection_mats, precision=highest)
        own_weight = jnp.broadcast_to(fock_value[orbital][None, :], (total, PARTNERS))
        weights = jnp.concatenate([own_weight, fock_value], axis=1)
        coupling = jnp.einsum("jn,jnad->jad", weights, sandwich, precision=highest)
        energies = virtual_energy[orbital]
        shift = energies[:, :, None] + energies[:, None, :] - occupied_energy[orbital] - occupied_energy[:, None, None]
        result = exchange_part + shift * matrices[orbital].astype(jnp.float32) - coupling
        count = kept_count[orbital][:, None, None]
        keep = (levels[None, :, None] < count) & (levels[None, None, :] < count)
        return jnp.where(keep, result, jnp.zeros_like(result)).reshape(total, NPNO * NPNO)

    return lax.map(one_row, jnp.arange(total, dtype=jnp.int32))
```

```python
import jax
import jax.numpy as jnp
from jax import lax
from jax.experimental import pallas as pl
from jax.experimental.pallas import tpu as pltpu
from jax.sharding import PartitionSpec as P

AUX = 512
PAO = 256
NPNO = 64
DOMAIN = 3
PARTNERS = 4
HALF = PAO // 2
MESH = pl.DeviceIdType.MESH
F32 = jnp.float32
BF16 = jnp.bfloat16


def passed_along(block, axis, distance):
    devices = range(lax.axis_size(axis))
    route = [(i - distance, i) for i in devices if i - distance in devices]
    return lax.ppermute(block, axis, route)


def remote(src, dst, send_sem, recv_sem, row, col):
    return pltpu.make_async_remote_copy(
        src_ref=src,
        dst_ref=dst,
        send_sem=send_sem,
        recv_sem=recv_sem,
        device_id={"row": row, "col": col},
        device_id_type=MESH,
    )


def arrived(ref, sem):
    pltpu.make_async_copy(ref, ref, sem).wait()


def each(count, body):
    def step(index, carry):
        body(index)
        return carry

    lax.fori_loop(0, count, step, 0)


def exchange(
    rows,
    cols,
    i_dev,
    j_dev,
    per_dev,
    orbital_atoms,
    fitting,
    coefficients,
    k_ref,
    coef,
    coef_left,
    total,
    metric,
    send_one,
    row_one,
    col_one,
    col_pick,
    row_all,
    col_all,
    coef_sem,
    send_row_sem,
    recv_row_sem,
    send_col_sem,
    recv_col_sem,
    gather_row_sem,
    gathered_row_sem,
    share_sem,
    gather_col_sem,
    gathered_col_sem,
):
    row = lax.axis_index("row")
    col = lax.axis_index("col")
    core = lax.rem(col, 2)
    sibling = col + 1 - 2 * core
    row_atoms = cols * per_dev

    barrier = pltpu.get_barrier_semaphore()

    def signal(row_id, col_id):
        pl.semaphore_signal(
            barrier, inc=1, device_id={"row": row_id, "col": col_id}, device_id_type=MESH
        )

    def greet(other):
        @pl.when(other != col)
        def _():
            signal(row, other)

        @pl.when(other != row)
        def _():
            signal(other, col)

        @pl.when((col != row) | (other != col))
        def _():
            signal(col, other)

    each(cols, greet)

    for i in range(i_dev):
        pltpu.make_async_copy(coefficients.at[i], coef.at[i], coef_sem.at[i]).start()

    above = lax.broadcasted_iota(jnp.int32, (HALF, HALF), 0)
    across = lax.broadcasted_iota(jnp.int32, (HALF, HALF), 1)
    lower = above > across
    upper = above < across
    on = above == across
    tile_row = lax.broadcasted_iota(jnp.int32, (16, HALF), 0)
    diagonal = jnp.zeros((16, HALF), F32)
    for a in range(per_dev):
        block = fitting[a]
        square = lax.dot_general(
            block, block, (((0,), (0,)), ((), ())), preferred_element_type=F32
        )
        first = square[:HALF, :HALF]
        last = square[HALF:, HALF:]
        triangles = jnp.where(lower, first, jnp.where(upper, last, 0.0)).astype(BF16)
        cross = square[:HALF, HALF:].astype(BF16)
        for d in range(cols // 2):
            send_one[d, a] = triangles[16 * d : 16 * d + 16]
            send_one[cols // 2 + d, a] = cross[16 * d : 16 * d + 16]
        for part, piece in ((0, first), (1, last)):
            line = jnp.sum(jnp.where(on, piece, 0.0), axis=0, keepdims=True)
            diagonal = jnp.where(tile_row == 2 * a + part, line, diagonal)
    for d in range(cols):
        send_one[d, per_dev] = diagonal.astype(BF16)

    pl.semaphore_wait(
        barrier, cols - 1 + rows - 1 + cols - jnp.where(row == col, 1, 0)
    )

    def first_row(d):
        return remote(
            send_one.at[d], row_one.at[col], send_row_sem.at[d], recv_row_sem.at[col], row, d
        )

    def first_col(d):
        return remote(
            send_one.at[d], col_one.at[col], send_col_sem.at[d], recv_col_sem.at[col], d, row
        )

    def own_row():
        return pltpu.make_async_copy(send_one.at[col], row_one.at[col], recv_row_sem.at[col])

    def own_col():
        return pltpu.make_async_copy(send_one.at[row], col_one.at[col], recv_col_sem.at[col])

    def start_first(step):
        to_col = lax.rem(row + step, rows)

        @pl.when((col != row) | (to_col != row))
        def _():
            first_col(to_col).start()

        to_row = lax.rem(col + step, cols)

        @pl.when(to_row != col)
        def _():
            first_row(to_row).start()

    each(cols, start_first)
    own_row().start()

    @pl.when(row == col)
    def _():
        own_col().start()

    for i in range(i_dev):
        pltpu.make_async_copy(coefficients.at[i], coef.at[i], coef_sem.at[i]).wait()

    def turn(index):
        i = lax.div(index, j_dev)
        j = lax.rem(index, j_dev)
        for s in range(2 * DOMAIN):
            coef_left[i, j, s] = jnp.transpose(coef[i, j, s])[:NPNO]
        total[index] = jnp.zeros((NPNO, 2 * NPNO), F32)

    each(i_dev * j_dev, turn)

    each(cols, lambda source: arrived(col_one.at[source], recv_col_sem.at[source]))

    def wanted(owner, slot):
        orbital = owner * i_dev + lax.div(slot, DOMAIN)
        atom = orbital_atoms[orbital, lax.rem(slot, DOMAIN)] - owner * row_atoms
        atom = jnp.clip(atom, 0, row_atoms - 1)
        return lax.div(atom, per_dev), lax.rem(atom, per_dev)

    def pick_col(slot):
        source, place = wanted(col, slot)
        col_pick[slot] = col_one[source, place]

    each(j_dev * DOMAIN, pick_col)

    def gather_col(other):
        return remote(
            col_pick, col_all.at[row], gather_col_sem.at[other], gathered_col_sem.at[row], other, col
        )

    def start_col(step):
        gather_col(lax.rem(row + 1 + step, rows)).start()

    each(rows - 1, start_col)
    own = pltpu.make_async_copy(col_pick, col_all.at[row], gathered_col_sem.at[row])
    own.start()

    each(cols, lambda source: arrived(row_one.at[source], recv_row_sem.at[source]))

    def pick_row(slot):
        source, place = wanted(row, slot)
        row_all[col, slot] = row_one[source, place]

    each(i_dev * DOMAIN, pick_row)

    def gather_row(other):
        return remote(
            row_all.at[col], row_all.at[col], gather_row_sem.at[other], gathered_row_sem.at[col], row, other
        )

    def share_row(source):
        return remote(
            row_all.at[source], row_all.at[source], share_sem.at[source], gathered_row_sem.at[source], row, sibling
        )

    gather_row(sibling).start()

    def peer(step):
        return lax.rem(col + 2 * (step + 1), cols)

    each(cols // 2 - 1, lambda step: gather_row(peer(step)).start())

    def share(step):
        source = peer(step)
        arrived(row_all.at[source], gathered_row_sem.at[source])
        share_row(source).start()

    each(cols // 2 - 1, share)

    def from_sibling(step):
        source = lax.rem(sibling + 2 * step, cols)
        arrived(row_all.at[source], gathered_row_sem.at[source])

    each(cols // 2, from_sibling)

    def build(held, one, owner, slot):
        packed = held[:, slot].reshape(PAO, HALF)
        source, place = wanted(owner, slot)
        lines = one[source, per_dev].astype(F32)
        first_line = jnp.where(place == 0, lines[0:1], lines[2:3])
        last_line = jnp.where(place == 0, lines[1:2], lines[3:4])
        triangles = packed[:HALF].astype(F32)
        turned = jnp.transpose(triangles)
        cross = packed[HALF:].astype(F32)
        first = jnp.where(lower, triangles, jnp.where(upper, turned, first_line))
        last = jnp.where(upper, triangles, jnp.where(lower, turned, last_line))
        metric[:HALF, :HALF] = first.astype(BF16)
        metric[:HALF, HALF:] = cross.astype(BF16)
        metric[HALF:, :HALF] = jnp.transpose(cross).astype(BF16)
        metric[HALF:, HALF:] = last.astype(BF16)

    def apply(i, j, s):
        mapped = jnp.dot(metric[...], coef[i, j, s], preferred_element_type=F32).astype(BF16)
        total[i * j_dev + j] += jnp.dot(
            coef_left[i, j, s], mapped, preferred_element_type=F32
        )

    def row_slot(slot):
        build(row_all, row_one, row, slot)
        for j in range(j_dev):
            apply(lax.div(slot, DOMAIN), j, lax.rem(slot, DOMAIN))

    each(i_dev * DOMAIN, row_slot)

    each(rows, lambda source: arrived(col_all.at[source], gathered_col_sem.at[source]))

    def col_slot(slot):
        build(col_all, col_one, col, slot)
        for i in range(i_dev):
            apply(i, lax.div(slot, DOMAIN), DOMAIN + lax.rem(slot, DOMAIN))

    each(j_dev * DOMAIN, col_slot)

    k_ref[...] = total[...]

    def finish_first(step):
        to_col = lax.rem(row + step, rows)

        @pl.when((col != row) | (to_col != row))
        def _():
            first_col(to_col).wait_send()

        to_row = lax.rem(col + step, cols)

        @pl.when(to_row != col)
        def _():
            first_row(to_row).wait_send()

    each(cols, finish_first)
    each(rows - 1, lambda step: gather_col(lax.rem(row + 1 + step, rows)).wait_send())
    gather_row(sibling).wait_send()
    each(cols // 2 - 1, lambda step: gather_row(peer(step)).wait_send())
    each(cols // 2 - 1, lambda step: share_row(peer(step)).wait_send())


def exchange_part_of(fitting, coefficients, orbital_atoms):
    rows = lax.axis_size("row")
    cols = lax.axis_size("col")
    i_dev, j_dev = coefficients.shape[:2]
    per_dev = fitting.shape[0]
    slots = i_dev * DOMAIN

    def body(*refs):
        exchange(rows, cols, i_dev, j_dev, per_dev, *refs)

    dma = pltpu.SemaphoreType.DMA
    slices = (per_dev + 1, 16, HALF)
    out = pl.pallas_call(
        body,
        out_shape=jax.ShapeDtypeStruct((i_dev * j_dev, NPNO, 2 * NPNO), F32),
        in_specs=[
            pl.BlockSpec(memory_space=pltpu.SMEM),
            pl.BlockSpec(memory_space=pltpu.VMEM),
            pl.BlockSpec(memory_space=pl.ANY),
        ],
        out_specs=pl.BlockSpec(memory_space=pltpu.VMEM),
        scratch_shapes=[
            pltpu.VMEM(coefficients.shape, BF16),
            pltpu.VMEM((i_dev, j_dev, 2 * DOMAIN, NPNO, PAO), BF16),
            pltpu.VMEM((i_dev * j_dev, NPNO, 2 * NPNO), F32),
            pltpu.VMEM((PAO, PAO), BF16),
            pltpu.VMEM((cols,) + slices, BF16),
            pltpu.VMEM((cols,) + slices, BF16),
            pltpu.VMEM((cols,) + slices, BF16),
            pltpu.VMEM((slots, 16, HALF), BF16),
            pltpu.VMEM((cols, slots, 16, HALF), BF16),
            pltpu.VMEM((rows, slots, 16, HALF), BF16),
            dma((i_dev,)),
            dma((cols,)),
            dma((cols,)),
            dma((rows,)),
            dma((cols,)),
            dma((cols,)),
            dma((cols,)),
            dma((cols,)),
            dma((rows,)),
            dma((rows,)),
        ],
        compiler_params=pltpu.CompilerParams(
            collective_id=0, has_side_effects=True, vmem_limit_bytes=48 * 1024 * 1024
        ),
        name="exchange",
    )(orbital_atoms, fitting, coefficients)
    return out.reshape(i_dev, j_dev, NPNO, 2 * NPNO)[..., NPNO:]


def on_device(
    fitting,
    coefficients,
    amplitudes,
    intersections,
    virtual_energy,
    occupied_energy,
    kept_count,
    orbital_atoms,
    fock_partner,
    fock_value,
):
    row_count = amplitudes.shape[0]
    column_count = amplitudes.shape[1]
    row_place = lax.axis_index("row")
    column_place = lax.axis_index("col")
    first_row = row_place * row_count
    first_column = column_place * column_count
    exchange_part = exchange_part_of(fitting, coefficients, orbital_atoms)
    exchange_part = exchange_part * (2 * DOMAIN * AUX) ** (-0.5)
    row_partner = lax.dynamic_slice_in_dim(fock_partner, first_row, row_count, 0)
    column_partner = lax.dynamic_slice_in_dim(fock_partner, first_column, column_count, 0)
    below_rows = passed_along(amplitudes, "row", 1)
    above_rows = passed_along(amplitudes, "row", -1)
    row_source = jnp.concatenate([below_rows, amplitudes, above_rows], axis=0)
    below_columns = passed_along(amplitudes, "col", 1)
    above_columns = passed_along(amplitudes, "col", -1)
    column_source = jnp.concatenate([below_columns, amplitudes, above_columns], axis=1)
    row_pick = row_partner - (first_row - column_count)
    column_pick = column_partner - (first_column - column_count)
    from_rows = jnp.transpose(jnp.take(row_source, row_pick, axis=0), (0, 2, 1, 3))
    from_columns = jnp.take(column_source, column_pick, axis=1)
    partners = jnp.concatenate([from_rows, from_columns], axis=2).reshape(
        row_count, column_count, 2 * PARTNERS, NPNO, NPNO
    )
    intersection_mats = intersections.reshape(row_count, column_count, 2 * PARTNERS, NPNO, NPNO)
    half = jnp.einsum(
        "ijnab,ijnbc->ijnac", intersection_mats, partners, preferred_element_type=jnp.float32
    ).astype(jnp.bfloat16)
    sandwich = jnp.einsum(
        "ijnac,ijndc->ijnad", half, intersection_mats, preferred_element_type=jnp.float32
    )
    row_weight = lax.dynamic_slice_in_dim(fock_value, first_row, row_count, 0)
    column_weight = lax.dynamic_slice_in_dim(fock_value, first_column, column_count, 0)
    weights = jnp.concatenate(
        [
            jnp.broadcast_to(row_weight[:, None, :], (row_count, column_count, PARTNERS)),
            jnp.broadcast_to(column_weight[None, :, :], (row_count, column_count, PARTNERS)),
        ],
        axis=2,
    )
    coupling = jnp.einsum("ijn,ijnad->ijad", weights, sandwich)
    row_occupied = lax.dynamic_slice_in_dim(occupied_energy, first_row, row_count, 0)
    column_occupied = lax.dynamic_slice_in_dim(occupied_energy, first_column, column_count, 0)
    shift = (
        virtual_energy[:, :, :, None]
        + virtual_energy[:, :, None, :]
        - row_occupied[:, None, None, None]
        - column_occupied[None, :, None, None]
    )
    current = amplitudes.reshape(row_count, column_count, NPNO, NPNO).astype(jnp.float32)
    result = exchange_part + shift * current - coupling
    levels = jnp.arange(NPNO, dtype=jnp.int32)
    count = kept_count[:, :, None, None]
    keep = (levels[None, None, :, None] < count) & (levels[None, None, None, :] < count)
    masked = jnp.where(keep, result, jnp.zeros_like(result))
    return masked.reshape(row_count, column_count, NPNO * NPNO)


def solution(mesh):
    placed = (
        P(("row", "col"), None, None),
        P("row", "col", None, None, None),
        P("row", "col", None),
        P("row", "col", None, None),
        P("row", "col", None),
        P(),
        P("row", "col"),
        P(),
        P(),
        P(),
    )
    return jax.shard_map(
        on_device, mesh=mesh, in_specs=placed, out_specs=P("row", "col", None), check_vma=False
    )
```

```python
import jax
import jax.numpy as jnp
from jax import lax
from jax.experimental import pallas as pl
from jax.experimental.pallas import tpu as pltpu
from jax.sharding import PartitionSpec as P

AUX = 512
PAO = 256
NPNO = 64
DOMAIN = 3
PARTNERS = 4
HALF = PAO // 2
MESH = pl.DeviceIdType.MESH
SKIP = frozenset()
F32 = jnp.float32
BF16 = jnp.bfloat16


SUB = 8
LANES = 128
PAIR = 2 * NPNO
CHUNKS = NPNO * NPNO // LANES


def remote(src, dst, send_sem, recv_sem, row, col):
    return pltpu.make_async_remote_copy(
        src_ref=src,
        dst_ref=dst,
        send_sem=send_sem,
        recv_sem=recv_sem,
        device_id={"row": row, "col": col},
        device_id_type=MESH,
    )


def arrived(ref, sem):
    pltpu.make_async_copy(ref, ref, sem).wait()


def each(count, body):
    def step(index, carry):
        body(index)
        return carry

    lax.fori_loop(0, count, step, 0)


def swap_halves(value):
    return pltpu.roll(value, NPNO, 1)


def low_lanes(shape):
    return lax.broadcasted_iota(jnp.int32, shape, 1) % LANES < NPNO


def join(first, second):
    low = low_lanes(first.shape)
    left = jnp.where(low, first, swap_halves(second))
    right = jnp.where(low, swap_halves(first), second)
    return left, right


def spread(block, scratch):
    count = block.shape[0]
    for k in range(CHUNKS):
        scratch[SUB * k : SUB * k + count, :] = block[:, LANES * k : LANES * k + LANES].astype(F32)


def packed_of(scratch, n):
    return scratch[pl.ds(n, CHUNKS, stride=SUB), :]


def twice_on_diagonal(packed, scratch):
    scratch[pl.ds(0, CHUNKS, stride=2), :] = packed
    scratch[pl.ds(1, CHUNKS, stride=2), :] = swap_halves(packed)
    rows = scratch[...]
    low = low_lanes(rows.shape)
    upper = jnp.where(low, rows, 0.0)
    lower = jnp.where(low, 0.0, swap_halves(rows))
    return jnp.concatenate([upper, lower], axis=0).astype(BF16)


def split_twice(packed):
    turned = swap_halves(packed)
    low = low_lanes(packed.shape)
    zero = jnp.zeros_like(packed)
    return jnp.concatenate(
        [
            jnp.where(low, packed, zero),
            jnp.where(low, turned, zero),
            jnp.where(low, zero, turned),
            jnp.where(low, zero, packed),
        ],
        axis=0,
    ).astype(BF16)


def residual_kernel(
    rows,
    cols,
    i_dev,
    j_dev,
    per_dev,
    orbital_atoms,
    fock_partner,
    fock_value,
    occupied,
    kept,
    fitting,
    amplitudes,
    energies,
    coefficients,
    intersections,
    out_ref,
    coef,
    inter,
    left_row,
    right_row,
    left_col,
    right_col,
    total_row,
    total_col,
    metric,
    send_one,
    relay,
    row_one,
    col_one,
    col_pick,
    row_all,
    col_all,
    halo,
    source_row,
    source_col,
    current,
    coupled,
    spread_scr,
    rows_scr,
    coef_sem,
    inter_sem,
    send_row_sem,
    recv_row_sem,
    send_relay_sem,
    recv_relay_sem,
    send_col_sem,
    recv_col_sem,
    gather_row_sem,
    gathered_row_sem,
    share_sem,
    gather_col_sem,
    gathered_col_sem,
    send_halo_sem,
    recv_halo_sem,
):
    row = lax.axis_index("row")
    col = lax.axis_index("col")
    core = lax.rem(col, 2)
    sibling = col + 1 - 2 * core
    row_atoms = cols * per_dev
    slots = i_dev * DOMAIN

    barrier = pltpu.get_barrier_semaphore()

    def greet(step):
        other = lax.rem(row + 1 + step, rows)
        pl.semaphore_signal(
            barrier, inc=1, device_id={"row": other, "col": col}, device_id_type=MESH
        )
        other = lax.rem(col + 1 + step, cols)
        pl.semaphore_signal(
            barrier, inc=1, device_id={"row": row, "col": other}, device_id_type=MESH
        )

    each(rows - 1, greet)

    def load_coef(i):
        return pltpu.make_async_copy(coefficients.at[i], coef.at[i], coef_sem.at[i])

    def load_inter(i):
        return pltpu.make_async_copy(intersections.at[i], inter.at[i], inter_sem.at[i])

    for i in range(i_dev):
        load_coef(i).start()
    for i in range(i_dev):
        load_inter(i).start()

    above = lax.broadcasted_iota(jnp.int32, (HALF, HALF), 0)
    across = lax.broadcasted_iota(jnp.int32, (HALF, HALF), 1)
    lower = above > across
    upper = above < across
    on = above == across
    tile_row = lax.broadcasted_iota(jnp.int32, (16, HALF), 0)
    diagonal = jnp.zeros((16, HALF), F32)
    for a in range(per_dev):
        block = fitting[a]
        square = lax.dot_general(
            block, block, (((0,), (0,)), ((), ())), preferred_element_type=F32
        )
        first = square[:HALF, :HALF]
        last = square[HALF:, HALF:]
        triangles = jnp.where(lower, first, jnp.where(upper, last, 0.0)).astype(BF16)
        cross = square[:HALF, HALF:].astype(BF16)
        for d in range(cols // 2):
            send_one[d, a] = triangles[16 * d : 16 * d + 16]
            send_one[cols // 2 + d, a] = cross[16 * d : 16 * d + 16]
        for part, piece in ((0, first), (1, last)):
            line = jnp.sum(jnp.where(on, piece, 0.0), axis=0, keepdims=True)
            diagonal = jnp.where(tile_row == 2 * a + part, line, diagonal)
    for d in range(cols):
        send_one[d, per_dev] = diagonal.astype(BF16)

    pl.semaphore_wait(barrier, cols - 1 + rows - 1)

    def to_plane(other):
        return remote(
            send_one.at[other], relay.at[row], send_relay_sem.at[other], recv_relay_sem.at[row], other, col
        )

    def to_row(other):
        return remote(
            send_one.at[other], row_one.at[col], send_row_sem.at[other], recv_row_sem.at[col], row, other
        )

    def to_col(other):
        return remote(
            relay.at[other], col_one.at[col], send_col_sem.at[other], recv_col_sem.at[col], row, other
        )

    def to_halo(place):
        other_row = lax.rem(row + (rows + 1, rows - 1, rows, rows)[place], rows)
        other_col = lax.rem(col + (cols, cols, cols + 1, cols - 1)[place], cols)
        return remote(
            amplitudes, halo.at[place], send_halo_sem.at[place], recv_halo_sem.at[place], other_row, other_col
        )

    def other_row(step):
        return lax.rem(row + 1 + step, rows)

    def other_col(step):
        return lax.rem(col + 1 + step, cols)

    def start_first(step):
        to_plane(other_row(step)).start()
        to_row(other_col(step)).start()

    each(rows - 1, start_first)
    pltpu.make_async_copy(send_one.at[row], relay.at[row], recv_relay_sem.at[row]).start()
    pltpu.make_async_copy(send_one.at[col], row_one.at[col], recv_row_sem.at[col]).start()
    for place in range(4):
        to_halo(place).start()

    def order_row(slot):
        i, s = lax.div(slot, DOMAIN), lax.rem(slot, DOMAIN)
        lefts, rights = [], []
        for j in range(0, j_dev, 2):
            left, right = join(coef[i, j, s], coef[i, j + 1, s])
            lefts.append(left)
            rights.append(right)
        left_row[slot] = jnp.transpose(jnp.concatenate(lefts, axis=1))
        right_row[slot] = jnp.concatenate(rights, axis=1)

    def order_col(slot):
        j, s = lax.div(slot, DOMAIN), DOMAIN + lax.rem(slot, DOMAIN)
        lefts, rights = [], []
        for i in range(0, i_dev, 2):
            left, right = join(coef[i, j, s], coef[i + 1, j, s])
            lefts.append(left)
            rights.append(right)
        left_col[slot] = jnp.transpose(jnp.concatenate(lefts, axis=1))
        right_col[slot] = jnp.concatenate(rights, axis=1)

    for i in range(i_dev):
        load_coef(i).wait()
    if "turn" not in SKIP:
        each(slots, order_row)

    def pass_on(step):
        other = other_row(step)
        arrived(relay.at[other], recv_relay_sem.at[other])

        @pl.when(other != col)
        def _():
            to_col(other).start()

        @pl.when(other == col)
        def _():
            pltpu.make_async_copy(relay.at[other], col_one.at[col], recv_col_sem.at[col]).start()

    each(rows, pass_on)

    each(cols, lambda source: arrived(row_one.at[source], recv_row_sem.at[source]))

    def wanted(owner, slot):
        orbital = owner * i_dev + lax.div(slot, DOMAIN)
        atom = orbital_atoms[orbital, lax.rem(slot, DOMAIN)] - owner * row_atoms
        atom = jnp.clip(atom, 0, row_atoms - 1)
        return lax.div(atom, per_dev), lax.rem(atom, per_dev)

    def pick_row(slot):
        source, place = wanted(row, slot)
        row_all[col, slot] = row_one[source, place]

    each(slots, pick_row)

    def gather_row(other):
        return remote(
            row_all.at[col], row_all.at[col], gather_row_sem.at[other], gathered_row_sem.at[col], row, other
        )

    def share_row(source):
        return remote(
            row_all.at[source], row_all.at[source], share_sem.at[source], gathered_row_sem.at[source], row, sibling
        )

    def peer(step):
        return lax.rem(col + 2 * (step + 1), cols)

    each(cols // 2 - 1, lambda step: gather_row(peer(step)).start())
    gather_row(sibling).start()

    if "turn" not in SKIP:
        each(slots, order_col)

    each(cols, lambda source: arrived(col_one.at[source], recv_col_sem.at[source]))

    def pick_col(slot):
        source, place = wanted(col, slot)
        col_pick[slot] = col_one[source, place]

    each(slots, pick_col)

    def gather_col(other):
        return remote(
            col_pick, col_all.at[row], gather_col_sem.at[other], gathered_col_sem.at[row], other, col
        )

    each(rows - 1, lambda step: gather_col(other_row(step)).start())
    pltpu.make_async_copy(col_pick, col_all.at[row], gathered_col_sem.at[row]).start()

    for place in range(4):
        arrived(halo.at[place], recv_halo_sem.at[place])

    def sources(place, block, first_row, first_col):
        def step(a):
            spread(block[a], spread_scr)
            for b in range(j_dev):
                packed = packed_of(spread_scr, b)
                twice = twice_on_diagonal(packed, rows_scr.at[b])
                if first_row is not None:
                    source_row[first_row + a, b] = twice
                if first_col is not None:
                    source_col[first_col + b, a] = twice
                if first_row is not None and first_col is not None:
                    current[a * j_dev + b] = packed

        each(i_dev, step)

    if "coup" not in SKIP:
        sources(0, amplitudes, i_dev, j_dev)
        sources(0, halo.at[0], 0, None)
        sources(0, halo.at[1], 2 * i_dev, None)
        sources(0, halo.at[2], None, 0)
        sources(0, halo.at[3], None, 2 * j_dev)

    for i in range(i_dev):
        load_inter(i).wait()

    def couple(index):
        i, j = lax.div(index, j_dev), lax.rem(index, j_dev)
        spread(inter[i, j], spread_scr)
        halves, squares = [], []
        for n in range(2 * PARTNERS):
            packed = packed_of(spread_scr, n)
            if n < PARTNERS:
                orbital = row * i_dev + i
                near = jnp.clip(fock_partner[orbital, n] - (row - 1) * i_dev, 0, 3 * i_dev - 1)
                partner = source_row[near, j]
                weight = fock_value[orbital, n]
            else:
                orbital = col * j_dev + j
                near = jnp.clip(
                    fock_partner[orbital, n - PARTNERS] - (col - 1) * j_dev, 0, 3 * j_dev - 1
                )
                partner = source_col[near, i]
                weight = fock_value[orbital, n - PARTNERS]
            half = jnp.dot(packed.astype(BF16), partner, preferred_element_type=F32)
            halves.append((half * weight).astype(BF16))
            squares.append(split_twice(packed))
        coupled[index] = lax.dot_general(
            jnp.concatenate(halves, axis=1),
            jnp.concatenate(squares, axis=1),
            (((1,), (1,)), ((), ())),
            preferred_element_type=F32,
        )

    if "coup" not in SKIP:
        each(i_dev * j_dev, couple)

    pick_from = lax.broadcasted_iota(jnp.int32, (LANES, LANES), 0)
    pick_to = lax.broadcasted_iota(jnp.int32, (LANES, LANES), 1)
    from_half, from_place = pick_from // NPNO, pick_from % NPNO
    ordered = from_half * NPNO + 2 * (from_place % (NPNO // 2)) + from_place // (NPNO // 2)
    order = jnp.where(ordered == pick_to, 1.0, 0.0).astype(BF16)
    at_row = 2 * lax.broadcasted_iota(jnp.int32, (CHUNKS, LANES), 0)
    at_lane = lax.broadcasted_iota(jnp.int32, (CHUNKS, LANES), 1)
    low = at_lane < NPNO
    level_a = at_row + jnp.where(low, 0, 1)
    level_b = jnp.where(low, at_lane, at_lane - NPNO)

    def local_part(index):
        i, j = lax.div(index, j_dev), lax.rem(index, j_dev)
        sums = coupled[index]
        high = sums.astype(BF16)
        rest = (sums - high.astype(F32)).astype(BF16)
        coupling = jnp.dot(high, order, preferred_element_type=F32) + jnp.dot(
            rest, order, preferred_element_type=F32
        )
        along = energies[pl.ds(index, 1), :]
        at_b = jnp.broadcast_to(along, (CHUNKS, LANES))
        even = jnp.sum(jnp.where(at_lane == at_row, at_b, 0.0), axis=1, keepdims=True)
        odd = jnp.sum(jnp.where(at_lane == at_row + 1, at_b, 0.0), axis=1, keepdims=True)
        shift = at_b + jnp.where(low, even, odd)
        shift = shift - occupied[row * i_dev + i] - occupied[col * j_dev + j]
        coupled[index] = shift * current[index] - coupling

    if "coup" not in SKIP:
        each(i_dev * j_dev, local_part)

    def share(step):
        source = peer(step)
        arrived(row_all.at[source], gathered_row_sem.at[source])
        share_row(source).start()

    each(cols // 2 - 1, share)

    def from_sibling(step):
        source = lax.rem(sibling + 2 * step, cols)
        arrived(row_all.at[source], gathered_row_sem.at[source])

    each(cols // 2, from_sibling)

    def build(held, one, owner, slot):
        packed = held[:, slot].reshape(PAO, HALF)
        source, place = wanted(owner, slot)
        lines = one[source, per_dev].astype(F32)
        first_line = jnp.where(place == 0, lines[0:1], lines[2:3])
        last_line = jnp.where(place == 0, lines[1:2], lines[3:4])
        triangles = packed[:HALF].astype(F32)
        turned = jnp.transpose(triangles)
        cross = packed[HALF:].astype(F32)
        first = jnp.where(lower, triangles, jnp.where(upper, turned, first_line))
        last = jnp.where(upper, triangles, jnp.where(lower, turned, last_line))
        metric[slot, :HALF, :HALF] = first.astype(BF16)
        metric[slot, :HALF, HALF:] = cross.astype(BF16)
        metric[slot, HALF:, :HALF] = jnp.transpose(cross).astype(BF16)
        metric[slot, HALF:, HALF:] = last.astype(BF16)

    def contract(left, right, total):
        def step(i):
            pieces = []
            for s in range(DOMAIN):
                slot = DOMAIN * i + s
                mapped = jnp.dot(metric[slot], right[slot], preferred_element_type=F32)
                pieces.append(
                    jnp.dot(left[slot], mapped.astype(BF16), preferred_element_type=F32)
                )
            whole = pieces[0] + pieces[1] + pieces[2]
            total[i, 0] = whole[:, :LANES]
            total[i, 1] = whole[:, LANES:]

        each(i_dev, step)

    def build_all(held, one, owner):
        def step(i):
            for s in range(DOMAIN):
                build(held, one, owner, DOMAIN * i + s)

        each(i_dev, step)

    if "build" not in SKIP:
        build_all(row_all, row_one, row)
    if "dots" not in SKIP:
        contract(left_row, right_row, total_row)

    each(rows, lambda source: arrived(col_all.at[source], gathered_col_sem.at[source]))

    if "build" not in SKIP:
        build_all(col_all, col_one, col)
    if "dots" not in SKIP:
        contract(left_col, right_col, total_col)

    def square_of(total, outer, inner):
        window = total.at[outer, inner // 2]
        even = window[pl.ds(NPNO * inner, CHUNKS, stride=2), :]
        odd = window[pl.ds(NPNO * inner + 1, CHUNKS, stride=2), :]
        if inner % 2 == 0:
            return jnp.where(low, even, swap_halves(odd))
        return jnp.where(low, swap_halves(even), odd)

    level = jnp.maximum(level_a, level_b)
    for i in range(i_dev):
        for j in range(j_dev):
            both = square_of(total_row, i, j) + square_of(total_col, j, i)
            result = both * (2 * DOMAIN * AUX) ** (-0.5) + coupled[i * j_dev + j]
            result = jnp.where(level < kept[i, j], result, 0.0)
            spread_scr[pl.ds(j, CHUNKS, stride=SUB), :] = result
        for k in range(CHUNKS):
            out_ref[i, :, LANES * k : LANES * k + LANES] = spread_scr[SUB * k : SUB * k + j_dev, :]

    def finish(step):
        to_plane(other_row(step)).wait_send()
        to_row(other_col(step)).wait_send()
        gather_col(other_row(step)).wait_send()
        to_col(other_col(step)).wait_send()

    each(rows - 1, finish)
    for place in range(4):
        to_halo(place).wait_send()
    gather_row(sibling).wait_send()
    each(cols // 2 - 1, lambda step: gather_row(peer(step)).wait_send())
    each(cols // 2 - 1, lambda step: share_row(peer(step)).wait_send())


def on_device(
    fitting,
    coefficients,
    amplitudes,
    intersections,
    virtual_energy,
    occupied_energy,
    kept_count,
    orbital_atoms,
    fock_partner,
    fock_value,
):
    rows = lax.axis_size("row")
    cols = lax.axis_size("col")
    i_dev, j_dev = coefficients.shape[:2]
    per_dev = fitting.shape[0]
    slots = i_dev * DOMAIN
    pairs = i_dev * j_dev
    energies = virtual_energy.reshape(pairs, NPNO)
    energies = jnp.concatenate([energies, energies], axis=1)

    def body(*refs):
        residual_kernel(rows, cols, i_dev, j_dev, per_dev, *refs)

    dma = pltpu.SemaphoreType.DMA
    slices = (per_dev + 1, 16, HALF)
    smem = pl.BlockSpec(memory_space=pltpu.SMEM)
    vmem = pl.BlockSpec(memory_space=pltpu.VMEM)
    hbm = pl.BlockSpec(memory_space=pl.ANY)
    return pl.pallas_call(
        body,
        out_shape=jax.ShapeDtypeStruct(amplitudes.shape, F32),
        in_specs=[smem] * 5 + [vmem] * 3 + [hbm] * 2,
        out_specs=vmem,
        scratch_shapes=[
            pltpu.VMEM(coefficients.shape, BF16),
            pltpu.VMEM(intersections.shape, BF16),
            pltpu.VMEM((slots, PAO, PAO), BF16),
            pltpu.VMEM((slots, PAO, PAO), BF16),
            pltpu.VMEM((slots, PAO, PAO), BF16),
            pltpu.VMEM((slots, PAO, PAO), BF16),
            pltpu.VMEM((i_dev, 2, PAO, LANES), F32),
            pltpu.VMEM((j_dev, 2, PAO, LANES), F32),
            pltpu.VMEM((slots, PAO, PAO), BF16),
            pltpu.VMEM((cols,) + slices, BF16),
            pltpu.VMEM((rows,) + slices, BF16),
            pltpu.VMEM((cols,) + slices, BF16),
            pltpu.VMEM((cols,) + slices, BF16),
            pltpu.VMEM((slots, 16, HALF), BF16),
            pltpu.VMEM((cols, slots, 16, HALF), BF16),
            pltpu.VMEM((rows, slots, 16, HALF), BF16),
            pltpu.VMEM((4,) + amplitudes.shape, BF16),
            pltpu.VMEM((3 * i_dev, j_dev, LANES, LANES), BF16),
            pltpu.VMEM((3 * j_dev, i_dev, LANES, LANES), BF16),
            pltpu.VMEM((pairs, CHUNKS, LANES), F32),
            pltpu.VMEM((pairs, CHUNKS, LANES), F32),
            pltpu.VMEM((SUB * CHUNKS, LANES), F32),
            pltpu.VMEM((j_dev, NPNO, LANES), F32),
            dma((i_dev,)),
            dma((i_dev,)),
        ]
        + [dma((rows,))] * 11
        + [dma((4,))] * 2,
        compiler_params=pltpu.CompilerParams(
            collective_id=0, has_side_effects=True, vmem_limit_bytes=56 * 1024 * 1024
        ),
        name="residual",
    )(
        orbital_atoms,
        fock_partner,
        fock_value,
        occupied_energy,
        kept_count,
        fitting,
        amplitudes,
        energies,
        coefficients,
        intersections,
    )


def solution(mesh):
    placed = (
        P(("row", "col"), None, None),
        P("row", "col", None, None, None),
        P("row", "col", None),
        P("row", "col", None, None),
        P("row", "col", None),
        P(),
        P("row", "col"),
        P(),
        P(),
        P(),
    )
    return jax.shard_map(
        on_device, mesh=mesh, in_specs=placed, out_specs=P("row", "col", None), check_vma=False
    )
```

```python
import jax
import jax.numpy as jnp
from jax import lax
from jax.experimental import pallas as pl
from jax.experimental.pallas import tpu as pltpu
from jax.sharding import PartitionSpec as P

AUX = 512
PAO = 256
NPNO = 64
DOMAIN = 3
PARTNERS = 4
HALF = PAO // 2
MESH = pl.DeviceIdType.MESH
SKIP = frozenset()
F32 = jnp.float32
BF16 = jnp.bfloat16


SUB = 8
EARLY_PAIRS = 4
PARTS = 2
LANES = 128
PAIR = 2 * NPNO
CHUNKS = NPNO * NPNO // LANES


def remote(src, dst, send_sem, recv_sem, row, col):
    return pltpu.make_async_remote_copy(
        src_ref=src,
        dst_ref=dst,
        send_sem=send_sem,
        recv_sem=recv_sem,
        device_id={"row": row, "col": col},
        device_id_type=MESH,
    )


def arrived(ref, sem):
    pltpu.make_async_copy(ref, ref, sem).wait()


def each(count, body):
    def step(index, carry):
        body(index)
        return carry

    lax.fori_loop(0, count, step, 0)


def swap_halves(value):
    return pltpu.roll(value, NPNO, 1)


def low_lanes(shape):
    return lax.broadcasted_iota(jnp.int32, shape, 1) % LANES < NPNO


def join(first, second):
    low = low_lanes(first.shape)
    left = jnp.where(low, first, swap_halves(second))
    right = jnp.where(low, swap_halves(first), second)
    return left, right


def spread(block, scratch):
    count = block.shape[0]
    for k in range(CHUNKS):
        scratch[SUB * k : SUB * k + count, :] = block[:, LANES * k : LANES * k + LANES].astype(F32)


def packed_of(scratch, n):
    return scratch[pl.ds(n, CHUNKS, stride=SUB), :]


def twice_on_diagonal(packed, scratch):
    scratch[pl.ds(0, CHUNKS, stride=2), :] = packed
    scratch[pl.ds(1, CHUNKS, stride=2), :] = swap_halves(packed)
    rows = scratch[...]
    low = low_lanes(rows.shape)
    upper = jnp.where(low, rows, 0.0)
    lower = jnp.where(low, 0.0, swap_halves(rows))
    return jnp.concatenate([upper, lower], axis=0).astype(BF16)


def split_twice(packed):
    turned = swap_halves(packed)
    low = low_lanes(packed.shape)
    zero = jnp.zeros_like(packed)
    return jnp.concatenate(
        [
            jnp.where(low, packed, zero),
            jnp.where(low, turned, zero),
            jnp.where(low, zero, turned),
            jnp.where(low, zero, packed),
        ],
        axis=0,
    ).astype(BF16)


def residual_kernel(
    rows,
    cols,
    i_dev,
    j_dev,
    per_dev,
    orbital_atoms_hbm,
    fock_partner_hbm,
    fock_value_hbm,
    occupied_hbm,
    kept_hbm,
    fitting_hbm,
    amplitudes_hbm,
    energies_hbm,
    coefficients,
    intersections,
    out_hbm,
    orbital_atoms,
    fock_partner,
    fock_value,
    occupied,
    kept,
    fitting,
    amplitudes,
    energies,
    out_ref,
    coef,
    inter,
    left_row,
    right_row,
    left_col,
    right_col,
    total_row,
    total_col,
    metric,
    send_one,
    relay,
    row_one,
    col_one,
    col_pick,
    row_all,
    col_all,
    halo,
    source_row,
    source_col,
    current,
    coupled,
    spread_scr,
    rows_scr,
    coef_sem,
    inter_sem,
    send_row_sem,
    recv_row_sem,
    send_relay_sem,
    recv_relay_sem,
    send_col_sem,
    recv_col_sem,
    gather_row_sem,
    gathered_row_sem,
    share_sem,
    gather_col_sem,
    gathered_col_sem,
    send_halo_sem,
    recv_halo_sem,
    load_sem,
    out_sem,
):
    row = lax.axis_index("row")
    col = lax.axis_index("col")
    core = lax.rem(col, 2)
    sibling = col + 1 - 2 * core
    row_atoms = cols * per_dev
    slots = i_dev * DOMAIN

    barrier = pltpu.get_barrier_semaphore()

    def greet(step):
        other = lax.rem(row + 1 + step, rows)
        pl.semaphore_signal(
            barrier, inc=1, device_id={"row": other, "col": col}, device_id_type=MESH
        )
        other = lax.rem(col + 1 + step, cols)
        pl.semaphore_signal(
            barrier, inc=1, device_id={"row": row, "col": other}, device_id_type=MESH
        )

    load_fitting = pltpu.make_async_copy(fitting_hbm, fitting, load_sem.at[0])
    load_amplitudes = pltpu.make_async_copy(amplitudes_hbm, amplitudes, load_sem.at[1])
    load_energies = pltpu.make_async_copy(energies_hbm, energies, load_sem.at[2])
    tables = [
        pltpu.make_async_copy(source, table, load_sem.at[3 + k])
        for k, (source, table) in enumerate(
            (
                (orbital_atoms_hbm, orbital_atoms),
                (fock_partner_hbm, fock_partner),
                (fock_value_hbm, fock_value),
                (occupied_hbm, occupied),
                (kept_hbm, kept),
            )
        )
    ]
    load_fitting.start()
    each(rows - 1, greet)
    for table in tables:
        table.start()
    load_amplitudes.start()
    load_energies.start()

    def load_coef(i):
        return pltpu.make_async_copy(coefficients.at[i], coef.at[i], coef_sem.at[i])

    def load_inter(i):
        return pltpu.make_async_copy(intersections.at[i], inter.at[i], inter_sem.at[i])

    for i in range(i_dev):
        load_coef(i).start()
    for i in range(i_dev):
        load_inter(i).start()

    above = lax.broadcasted_iota(jnp.int32, (HALF, HALF), 0)
    across = lax.broadcasted_iota(jnp.int32, (HALF, HALF), 1)
    lower = above > across
    upper = above < across
    on = above == across
    tile_row = lax.broadcasted_iota(jnp.int32, (16, HALF), 0)
    diagonal = jnp.zeros((16, HALF), F32)
    load_fitting.wait()
    load_amplitudes.wait()
    load_energies.wait()
    for table in tables:
        table.wait()
    for a in range(per_dev):
        block = fitting[a]
        square = lax.dot_general(
            block, block, (((0,), (0,)), ((), ())), preferred_element_type=F32
        )
        first = square[:HALF, :HALF]
        last = square[HALF:, HALF:]
        triangles = jnp.where(lower, first, jnp.where(upper, last, 0.0)).astype(BF16)
        cross = square[:HALF, HALF:].astype(BF16)
        for d in range(cols // 2):
            send_one[d, a] = triangles[16 * d : 16 * d + 16]
            send_one[cols // 2 + d, a] = cross[16 * d : 16 * d + 16]
        for part, piece in ((0, first), (1, last)):
            line = jnp.sum(jnp.where(on, piece, 0.0), axis=0, keepdims=True)
            diagonal = jnp.where(tile_row == 2 * a + part, line, diagonal)
    for d in range(cols):
        send_one[d, per_dev] = diagonal.astype(BF16)

    pl.semaphore_wait(barrier, cols - 1 + rows - 1)

    def to_plane(other):
        return remote(
            send_one.at[other], relay.at[row], send_relay_sem.at[other], recv_relay_sem.at[row], other, col
        )

    def to_row(other):
        return remote(
            send_one.at[other], row_one.at[col], send_row_sem.at[other], recv_row_sem.at[col], row, other
        )

    def to_col(other):
        return remote(
            relay.at[other], col_one.at[col], send_col_sem.at[other], recv_col_sem.at[col], row, other
        )

    def to_halo(place):
        other_row = lax.rem(row + (rows + 1, rows - 1, rows, rows)[place], rows)
        other_col = lax.rem(col + (cols, cols, cols + 1, cols - 1)[place], cols)
        return remote(
            amplitudes, halo.at[place], send_halo_sem.at[place], recv_halo_sem.at[place], other_row, other_col
        )

    def other_row(step):
        return lax.rem(row + 1 + step, rows)

    def other_col(step):
        return lax.rem(col + 1 + step, cols)

    def start_first(step):
        to_plane(other_row(step)).start()
        to_row(other_col(step)).start()

    each(rows - 1, start_first)
    pltpu.make_async_copy(send_one.at[row], relay.at[row], recv_relay_sem.at[row]).start()
    pltpu.make_async_copy(send_one.at[col], row_one.at[col], recv_row_sem.at[col]).start()
    for place in range(4):
        to_halo(place).start()

    def order_row(slot):
        i, s = lax.div(slot, DOMAIN), lax.rem(slot, DOMAIN)
        lefts, rights = [], []
        for j in range(0, j_dev, 2):
            left, right = join(coef[i, j, s], coef[i, j + 1, s])
            lefts.append(left)
            rights.append(right)
        left_row[slot] = jnp.transpose(jnp.concatenate(lefts, axis=1))
        right_row[slot] = jnp.concatenate(rights, axis=1)

    def order_col(slot):
        j, s = lax.div(slot, DOMAIN), DOMAIN + lax.rem(slot, DOMAIN)
        lefts, rights = [], []
        for i in range(0, i_dev, 2):
            left, right = join(coef[i, j, s], coef[i + 1, j, s])
            lefts.append(left)
            rights.append(right)
        left_col[slot] = jnp.transpose(jnp.concatenate(lefts, axis=1))
        right_col[slot] = jnp.concatenate(rights, axis=1)

    for i in range(i_dev):
        load_coef(i).wait()
    if "turn" not in SKIP:
        each(slots, order_row)
        each(slots, order_col)

    def pass_on(step):
        other = other_row(step)
        arrived(relay.at[other], recv_relay_sem.at[other])

        @pl.when(other != col)
        def _():
            to_col(other).start()

        @pl.when(other == col)
        def _():
            pltpu.make_async_copy(relay.at[other], col_one.at[col], recv_col_sem.at[col]).start()

    each(rows, pass_on)

    each(cols, lambda source: arrived(row_one.at[source], recv_row_sem.at[source]))

    def wanted(owner, slot):
        orbital = owner * i_dev + lax.div(slot, DOMAIN)
        atom = orbital_atoms[lax.rem(slot, DOMAIN), orbital] - owner * row_atoms
        atom = jnp.clip(atom, 0, row_atoms - 1)
        return lax.div(atom, per_dev), lax.rem(atom, per_dev)

    def pick_row(slot):
        source, place = wanted(row, slot)
        row_all[col, slot] = row_one[source, place]

    each(slots, pick_row)

    def part_of(ref, part):
        return ref.at[pl.ds(part * (slots // PARTS), slots // PARTS)]

    def gather_row(part, other):
        held = part_of(row_all.at[col], part)
        return remote(
            held, held, gather_row_sem.at[part, other], gathered_row_sem.at[part, col], row, other
        )

    def share_row(part, source):
        held = part_of(row_all.at[source], part)
        return remote(
            held, held, share_sem.at[part, source], gathered_row_sem.at[part, source], row, sibling
        )

    def row_arrived(part, source):
        arrived(part_of(row_all.at[source], part), gathered_row_sem.at[part, source])

    def peer(step):
        return lax.rem(col + 2 * (step + 1), cols)

    for part in range(PARTS):
        each(cols // 2 - 1, lambda step: gather_row(part, peer(step)).start())
        gather_row(part, sibling).start()

    for place in range(4):
        arrived(halo.at[place], recv_halo_sem.at[place])

    def sources(place, block, first_row, first_col):
        def step(a):
            spread(block[a], spread_scr)
            for b in range(j_dev):
                packed = packed_of(spread_scr, b)
                twice = twice_on_diagonal(packed, rows_scr.at[b])
                if first_row is not None:
                    source_row[first_row + a, b] = twice
                if first_col is not None:
                    source_col[first_col + b, a] = twice
                if first_row is not None and first_col is not None:
                    current[a * j_dev + b] = packed

        each(i_dev, step)

    if "coup" not in SKIP:
        sources(0, amplitudes, i_dev, j_dev)
        sources(0, halo.at[0], 0, None)
        sources(0, halo.at[1], 2 * i_dev, None)
        sources(0, halo.at[2], None, 0)
        sources(0, halo.at[3], None, 2 * j_dev)

    for i in range(i_dev):
        load_inter(i).wait()

    def couple(index):
        i, j = lax.div(index, j_dev), lax.rem(index, j_dev)
        spread(inter[i, j], spread_scr)
        halves, squares = [], []
        for n in range(2 * PARTNERS):
            packed = packed_of(spread_scr, n)
            if n < PARTNERS:
                orbital = row * i_dev + i
                near = jnp.clip(fock_partner[n, orbital] - (row - 1) * i_dev, 0, 3 * i_dev - 1)
                partner = source_row[near, j]
                weight = fock_value[n, orbital]
            else:
                orbital = col * j_dev + j
                near = jnp.clip(
                    fock_partner[n - PARTNERS, orbital] - (col - 1) * j_dev, 0, 3 * j_dev - 1
                )
                partner = source_col[near, i]
                weight = fock_value[n - PARTNERS, orbital]
            half = jnp.dot(packed.astype(BF16), partner, preferred_element_type=F32)
            halves.append((half * weight).astype(BF16))
            squares.append(split_twice(packed))
        coupled[index] = lax.dot_general(
            jnp.concatenate(halves, axis=1),
            jnp.concatenate(squares, axis=1),
            (((1,), (1,)), ((), ())),
            preferred_element_type=F32,
        )

    if "coup" not in SKIP:
        each(EARLY_PAIRS, couple)

    each(cols, lambda source: arrived(col_one.at[source], recv_col_sem.at[source]))

    def pick_col(slot):
        source, place = wanted(col, slot)
        col_pick[slot] = col_one[source, place]

    each(slots, pick_col)

    def gather_col(part, other):
        return remote(
            part_of(col_pick, part),
            part_of(col_all.at[row], part),
            gather_col_sem.at[part, other],
            gathered_col_sem.at[part, row],
            other,
            col,
        )

    def keep_col(part):
        return pltpu.make_async_copy(
            part_of(col_pick, part), part_of(col_all.at[row], part), gathered_col_sem.at[part, row]
        )

    def col_arrived(part, source):
        arrived(part_of(col_all.at[source], part), gathered_col_sem.at[part, source])

    for part in range(PARTS):
        each(rows - 1, lambda step: gather_col(part, other_row(step)).start())
        keep_col(part).start()

    if "coup" not in SKIP:
        each(i_dev * j_dev - EARLY_PAIRS, lambda index: couple(index + EARLY_PAIRS))

    pick_from = lax.broadcasted_iota(jnp.int32, (LANES, LANES), 0)
    pick_to = lax.broadcasted_iota(jnp.int32, (LANES, LANES), 1)
    from_half, from_place = pick_from // NPNO, pick_from % NPNO
    ordered = from_half * NPNO + 2 * (from_place % (NPNO // 2)) + from_place // (NPNO // 2)
    order = jnp.where(ordered == pick_to, 1.0, 0.0).astype(BF16)
    at_row = 2 * lax.broadcasted_iota(jnp.int32, (CHUNKS, LANES), 0)
    at_lane = lax.broadcasted_iota(jnp.int32, (CHUNKS, LANES), 1)
    low = at_lane < NPNO
    level_a = at_row + jnp.where(low, 0, 1)
    level_b = jnp.where(low, at_lane, at_lane - NPNO)

    def local_part(i, j, along):
        index = i * j_dev + j
        sums = coupled[index]
        high = sums.astype(BF16)
        rest = (sums - high.astype(F32)).astype(BF16)
        coupling = jnp.dot(high, order, preferred_element_type=F32) + jnp.dot(
            rest, order, preferred_element_type=F32
        )
        at_b = jnp.broadcast_to(jnp.concatenate([along, along], axis=1), (CHUNKS, LANES))
        even = jnp.sum(jnp.where(at_lane == at_row, at_b, 0.0), axis=1, keepdims=True)
        odd = jnp.sum(jnp.where(at_lane == at_row + 1, at_b, 0.0), axis=1, keepdims=True)
        shift = at_b + jnp.where(low, even, odd)
        shift = shift - occupied[row * i_dev + i] - occupied[col * j_dev + j]
        coupled[index] = shift * current[index] - coupling

    def local_row(i):
        levels = energies[i]
        for j in range(j_dev):
            local_part(i, j, levels[j : j + 1])

    if "coup" not in SKIP:
        each(i_dev, local_row)

    def share(part):
        def step(number):
            source = peer(number)
            row_arrived(part, source)
            share_row(part, source).start()

        each(cols // 2 - 1, step)

    def from_sibling(part):
        each(cols // 2, lambda step: row_arrived(part, lax.rem(sibling + 2 * step, cols)))

    def build(held, one, owner, slot):
        packed = held[:, slot].reshape(PAO, HALF)
        source, place = wanted(owner, slot)
        lines = one[source, per_dev].astype(F32)
        first_line = jnp.where(place == 0, lines[0:1], lines[2:3])
        last_line = jnp.where(place == 0, lines[1:2], lines[3:4])
        triangles = packed[:HALF].astype(F32)
        turned = jnp.transpose(triangles)
        cross = packed[HALF:].astype(F32)
        first = jnp.where(lower, triangles, jnp.where(upper, turned, first_line))
        last = jnp.where(upper, triangles, jnp.where(lower, turned, last_line))
        metric[slot, :HALF, :HALF] = first.astype(BF16)
        metric[slot, :HALF, HALF:] = cross.astype(BF16)
        metric[slot, HALF:, :HALF] = jnp.transpose(cross).astype(BF16)
        metric[slot, HALF:, HALF:] = last.astype(BF16)

    def contract(part, left, right, total):
        def step(i):
            pieces = []
            for s in range(DOMAIN):
                slot = DOMAIN * i + s
                mapped = jnp.dot(metric[slot], right[slot], preferred_element_type=F32)
                pieces.append(
                    jnp.dot(left[slot], mapped.astype(BF16), preferred_element_type=F32)
                )
            whole = pieces[0] + pieces[1] + pieces[2]
            total[i, 0] = whole[:, :LANES]
            total[i, 1] = whole[:, LANES:]

        each(i_dev // PARTS, lambda i: step(i + part * (i_dev // PARTS)))

    def build_all(part, held, one, owner):
        def step(i):
            for s in range(DOMAIN):
                build(held, one, owner, DOMAIN * i + s)

        each(i_dev // PARTS, lambda i: step(i + part * (i_dev // PARTS)))

    for part in range(PARTS):
        share(part)
    for part in range(PARTS):
        from_sibling(part)
        if "build" not in SKIP:
            build_all(part, row_all, row_one, row)
        if "dots" not in SKIP:
            contract(part, left_row, right_row, total_row)
    for part in range(PARTS):
        each(rows, lambda source: col_arrived(part, source))
        if "build" not in SKIP:
            build_all(part, col_all, col_one, col)
        if "dots" not in SKIP:
            contract(part, left_col, right_col, total_col)

    def square_of(total, outer, inner):
        window = total.at[outer, inner // 2]
        even = window[pl.ds(NPNO * inner, CHUNKS, stride=2), :]
        odd = window[pl.ds(NPNO * inner + 1, CHUNKS, stride=2), :]
        if inner % 2 == 0:
            return jnp.where(low, even, swap_halves(odd))
        return jnp.where(low, swap_halves(even), odd)

    def store_out(i):
        return pltpu.make_async_copy(out_ref.at[i], out_hbm.at[i], out_sem.at[i])

    level = jnp.maximum(level_a, level_b)
    for i in range(i_dev):
        for j in range(j_dev):
            both = square_of(total_row, i, j) + square_of(total_col, j, i)
            result = both * (2 * DOMAIN * AUX) ** (-0.5) + coupled[i * j_dev + j]
            result = jnp.where(level < kept[i, j], result, 0.0)
            spread_scr[pl.ds(j, CHUNKS, stride=SUB), :] = result
        for k in range(CHUNKS):
            out_ref[i, :, LANES * k : LANES * k + LANES] = spread_scr[SUB * k : SUB * k + j_dev, :]
        store_out(i).start()

    def finish(step):
        to_plane(other_row(step)).wait_send()
        to_row(other_col(step)).wait_send()
        for part in range(PARTS):
            gather_col(part, other_row(step)).wait_send()
        to_col(other_col(step)).wait_send()

    each(rows - 1, finish)
    for i in range(i_dev):
        store_out(i).wait()
    for place in range(4):
        to_halo(place).wait_send()
    for part in range(PARTS):
        gather_row(part, sibling).wait_send()

    def finish_row(step):
        for part in range(PARTS):
            gather_row(part, peer(step)).wait_send()
            share_row(part, peer(step)).wait_send()

    each(cols // 2 - 1, finish_row)


def on_device(
    fitting,
    coefficients,
    amplitudes,
    intersections,
    virtual_energy,
    occupied_energy,
    kept_count,
    orbital_atoms,
    fock_partner,
    fock_value,
):
    rows = lax.axis_size("row")
    cols = lax.axis_size("col")
    i_dev, j_dev = coefficients.shape[:2]
    per_dev = fitting.shape[0]
    slots = i_dev * DOMAIN
    pairs = i_dev * j_dev

    def body(*refs):
        residual_kernel(rows, cols, i_dev, j_dev, per_dev, *refs)

    dma = pltpu.SemaphoreType.DMA
    slices = (per_dev + 1, 16, HALF)
    hbm = pl.BlockSpec(memory_space=pl.ANY)
    return pl.pallas_call(
        body,
        out_shape=jax.ShapeDtypeStruct(amplitudes.shape, F32),
        in_specs=[hbm] * 10,
        out_specs=hbm,
        scratch_shapes=[
            pltpu.SMEM(orbital_atoms.shape[::-1], jnp.int32),
            pltpu.SMEM(fock_partner.shape[::-1], jnp.int32),
            pltpu.SMEM(fock_value.shape[::-1], F32),
            pltpu.SMEM(occupied_energy.shape, F32),
            pltpu.SMEM(kept_count.shape, jnp.int32),
            pltpu.VMEM(fitting.shape, BF16),
            pltpu.VMEM(amplitudes.shape, BF16),
            pltpu.VMEM(virtual_energy.shape, F32),
            pltpu.VMEM(amplitudes.shape, F32),
            pltpu.VMEM(coefficients.shape, BF16),
            pltpu.VMEM(intersections.shape, BF16),
            pltpu.VMEM((slots, PAO, PAO), BF16),
            pltpu.VMEM((slots, PAO, PAO), BF16),
            pltpu.VMEM((slots, PAO, PAO), BF16),
            pltpu.VMEM((slots, PAO, PAO), BF16),
            pltpu.VMEM((i_dev, 2, PAO, LANES), F32),
            pltpu.VMEM((j_dev, 2, PAO, LANES), F32),
            pltpu.VMEM((slots, PAO, PAO), BF16),
            pltpu.VMEM((cols,) + slices, BF16),
            pltpu.VMEM((rows,) + slices, BF16),
            pltpu.VMEM((cols,) + slices, BF16),
            pltpu.VMEM((cols,) + slices, BF16),
            pltpu.VMEM((slots, 16, HALF), BF16),
            pltpu.VMEM((cols, slots, 16, HALF), BF16),
            pltpu.VMEM((rows, slots, 16, HALF), BF16),
            pltpu.VMEM((4,) + amplitudes.shape, BF16),
            pltpu.VMEM((3 * i_dev, j_dev, LANES, LANES), BF16),
            pltpu.VMEM((3 * j_dev, i_dev, LANES, LANES), BF16),
            pltpu.VMEM((pairs, CHUNKS, LANES), F32),
            pltpu.VMEM((pairs, CHUNKS, LANES), F32),
            pltpu.VMEM((SUB * CHUNKS, LANES), F32),
            pltpu.VMEM((j_dev, NPNO, LANES), F32),
            dma((i_dev,)),
            dma((i_dev,)),
        ]
        + [dma((rows,))] * 6
        + [dma((PARTS, rows))] * 5
        + [dma((4,))] * 2
        + [dma((8,)), dma((i_dev,))],
        compiler_params=pltpu.CompilerParams(
            collective_id=0, has_side_effects=True, vmem_limit_bytes=62 * 1024 * 1024
        ),
        name="residual",
    )(
        orbital_atoms.T,
        fock_partner.T,
        fock_value.T,
        occupied_energy,
        kept_count,
        fitting,
        amplitudes,
        virtual_energy,
        coefficients,
        intersections,
    )


def solution(mesh):
    placed = (
        P(("row", "col"), None, None),
        P("row", "col", None, None, None),
        P("row", "col", None),
        P("row", "col", None, None),
        P("row", "col", None),
        P(),
        P("row", "col"),
        P(),
        P(),
        P(),
    )
    return jax.shard_map(
        on_device, mesh=mesh, in_specs=placed, out_specs=P("row", "col", None), check_vma=False
    )
```

```python
import jax
import jax.numpy as jnp
from jax import lax
from jax.experimental import pallas as pl
from jax.experimental.pallas import tpu as pltpu
from jax.sharding import PartitionSpec as P

AUX = 512
PAO = 256
NPNO = 64
DOMAIN = 3
PARTNERS = 4
HALF = PAO // 2
MESH = pl.DeviceIdType.MESH
SKIP = frozenset()
F32 = jnp.float32
BF16 = jnp.bfloat16


SUB = 8
EARLY_PAIRS = 4
PARTS = 2
PREPARED = 16
LANES = 128
PAIR = 2 * NPNO
CHUNKS = NPNO * NPNO // LANES


def remote(src, dst, send_sem, recv_sem, row, col):
    return pltpu.make_async_remote_copy(
        src_ref=src,
        dst_ref=dst,
        send_sem=send_sem,
        recv_sem=recv_sem,
        device_id={"row": row, "col": col},
        device_id_type=MESH,
    )


def arrived(ref, sem):
    pltpu.make_async_copy(ref, ref, sem).wait()


def each(count, body):
    def step(index, carry):
        body(index)
        return carry

    lax.fori_loop(0, count, step, 0)


def twice(count, body):
    def step(index):
        body(2 * index)
        body(2 * index + 1)

    each(count // 2, step)


def swap_halves(value):
    return pltpu.roll(value, NPNO, 1)


def low_lanes(shape):
    return lax.broadcasted_iota(jnp.int32, shape, 1) % LANES < NPNO


def join(first, second):
    low = low_lanes(first.shape)
    left = jnp.where(low, first, swap_halves(second))
    right = jnp.where(low, swap_halves(first), second)
    return left, right


def spread(block, scratch):
    count = block.shape[0]
    for k in range(CHUNKS):
        scratch[SUB * k : SUB * k + count, :] = block[:, LANES * k : LANES * k + LANES].astype(F32)


def packed_of(scratch, n):
    return scratch[pl.ds(n, CHUNKS, stride=SUB), :]


def twice_on_diagonal(packed, scratch):
    scratch[pl.ds(0, CHUNKS, stride=2), :] = packed
    scratch[pl.ds(1, CHUNKS, stride=2), :] = swap_halves(packed)
    rows = scratch[...]
    low = low_lanes(rows.shape)
    upper = jnp.where(low, rows, 0.0)
    lower = jnp.where(low, 0.0, swap_halves(rows))
    return jnp.concatenate([upper, lower], axis=0).astype(BF16)


def split_twice(packed):
    turned = swap_halves(packed)
    low = low_lanes(packed.shape)
    zero = jnp.zeros_like(packed)
    return jnp.concatenate(
        [
            jnp.where(low, packed, zero),
            jnp.where(low, turned, zero),
            jnp.where(low, zero, turned),
            jnp.where(low, zero, packed),
        ],
        axis=0,
    ).astype(BF16)


def residual_kernel(
    rows,
    cols,
    i_dev,
    j_dev,
    per_dev,
    orbital_atoms_hbm,
    fock_partner_hbm,
    fock_value_hbm,
    occupied_hbm,
    kept_hbm,
    fitting_hbm,
    amplitudes_hbm,
    energies_hbm,
    coefficients,
    intersections,
    out_hbm,
    orbital_atoms,
    fock_partner,
    fock_value,
    occupied,
    kept,
    fitting,
    amplitudes,
    energies,
    out_ref,
    coef,
    inter,
    left_row,
    right_row,
    left_col,
    right_col,
    total_row,
    total_col,
    metric,
    send_one,
    relay,
    row_one,
    col_one,
    col_pick,
    row_all,
    col_all,
    halo,
    source_row,
    source_col,
    current,
    coupled,
    spread_scr,
    rows_scr,
    lines_row,
    lines_col,
    flats,
    squares,
    more_scr,
    coef_sem,
    inter_sem,
    send_row_sem,
    recv_row_sem,
    send_relay_sem,
    recv_relay_sem,
    send_col_sem,
    recv_col_sem,
    gather_row_sem,
    gathered_row_sem,
    share_sem,
    gather_col_sem,
    gathered_col_sem,
    send_halo_sem,
    recv_halo_sem,
    load_sem,
    out_sem,
    send_lines_sem,
    recv_lines_sem,
):
    row = lax.axis_index("row")
    col = lax.axis_index("col")
    core = lax.rem(col, 2)
    sibling = col + 1 - 2 * core
    row_atoms = cols * per_dev
    slots = i_dev * DOMAIN

    barrier = pltpu.get_barrier_semaphore()

    def greet(step):
        other = lax.rem(row + 1 + step, rows)
        pl.semaphore_signal(
            barrier, inc=1, device_id={"row": other, "col": col}, device_id_type=MESH
        )
        other = lax.rem(col + 1 + step, cols)
        pl.semaphore_signal(
            barrier, inc=1, device_id={"row": row, "col": other}, device_id_type=MESH
        )

    load_fitting = pltpu.make_async_copy(fitting_hbm, fitting, load_sem.at[0])
    load_amplitudes = pltpu.make_async_copy(amplitudes_hbm, amplitudes, load_sem.at[1])
    load_energies = pltpu.make_async_copy(energies_hbm, energies, load_sem.at[2])
    tables = [
        pltpu.make_async_copy(source, table, load_sem.at[3 + k])
        for k, (source, table) in enumerate(
            (
                (orbital_atoms_hbm, orbital_atoms),
                (fock_partner_hbm, fock_partner),
                (fock_value_hbm, fock_value),
                (occupied_hbm, occupied),
                (kept_hbm, kept),
            )
        )
    ]
    load_fitting.start()
    each(rows - 1, greet)
    for table in tables:
        table.start()
    load_amplitudes.start()
    load_energies.start()

    def load_coef(i):
        return pltpu.make_async_copy(coefficients.at[i], coef.at[i], coef_sem.at[i])

    def load_inter(i):
        return pltpu.make_async_copy(intersections.at[i], inter.at[i], inter_sem.at[i])

    for i in range(i_dev):
        load_coef(i).start()
    for i in range(i_dev):
        load_inter(i).start()

    above = lax.broadcasted_iota(jnp.int32, (HALF, HALF), 0)
    across = lax.broadcasted_iota(jnp.int32, (HALF, HALF), 1)
    lower = above > across
    upper = above < across
    on = above == across
    tile_row = lax.broadcasted_iota(jnp.int32, (16, HALF), 0)
    diagonal = jnp.zeros((16, HALF), F32)
    load_fitting.wait()
    load_amplitudes.wait()
    load_energies.wait()
    for table in tables:
        table.wait()
    for a in range(per_dev):
        block = fitting[a]
        square = lax.dot_general(
            block, block, (((0,), (0,)), ((), ())), preferred_element_type=F32
        )
        first = square[:HALF, :HALF]
        last = square[HALF:, HALF:]
        triangles = jnp.where(upper, last, first).astype(BF16)
        cross = square[:HALF, HALF:].astype(BF16)
        for d in range(cols // 2):
            send_one[d, a] = triangles[16 * d : 16 * d + 16]
            send_one[cols // 2 + d, a] = cross[16 * d : 16 * d + 16]
        line = jnp.sum(jnp.where(on, last, 0.0), axis=0, keepdims=True)
        diagonal = jnp.where(tile_row == a, line, diagonal)
    for d in range(cols):
        send_one[d, per_dev] = diagonal.astype(BF16)

    pl.semaphore_wait(barrier, cols - 1 + rows - 1)

    def to_plane(other):
        return remote(
            send_one.at[other, pl.ds(0, per_dev)], relay.at[row], send_relay_sem.at[other], recv_relay_sem.at[row], other, col
        )

    def to_row(other):
        return remote(
            send_one.at[other], row_one.at[col], send_row_sem.at[other], recv_row_sem.at[col], row, other
        )

    def to_col(other):
        return remote(
            relay.at[other], col_one.at[col], send_col_sem.at[other], recv_col_sem.at[col], row, other
        )

    def to_halo(place):
        other_row = lax.rem(row + (rows + 1, rows - 1, rows, rows)[place], rows)
        other_col = lax.rem(col + (cols, cols, cols + 1, cols - 1)[place], cols)
        return remote(
            amplitudes, halo.at[place], send_halo_sem.at[place], recv_halo_sem.at[place], other_row, other_col
        )

    def other_row(step):
        return lax.rem(row + 1 + step, rows)

    def other_col(step):
        return lax.rem(col + 1 + step, cols)

    def start_first(step):
        to_plane(other_row(step)).start()
        to_row(other_col(step)).start()

    each(rows - 1, start_first)
    pltpu.make_async_copy(
        send_one.at[row, pl.ds(0, per_dev)], relay.at[row], recv_relay_sem.at[row]
    ).start()
    pltpu.make_async_copy(send_one.at[col], row_one.at[col], recv_row_sem.at[col]).start()
    for place in range(4):
        to_halo(place).start()

    def order_row(slot):
        i, s = lax.div(slot, DOMAIN), lax.rem(slot, DOMAIN)
        lefts, rights = [], []
        for j in range(0, j_dev, 2):
            left, right = join(coef[i, j, s], coef[i, j + 1, s])
            lefts.append(left)
            rights.append(right)
        left_row[slot] = jnp.transpose(jnp.concatenate(lefts, axis=1))
        right_row[slot] = jnp.concatenate(rights, axis=1)

    def order_col(slot):
        j, s = lax.div(slot, DOMAIN), DOMAIN + lax.rem(slot, DOMAIN)
        lefts, rights = [], []
        for i in range(0, i_dev, 2):
            left, right = join(coef[i, j, s], coef[i + 1, j, s])
            lefts.append(left)
            rights.append(right)
        left_col[slot] = jnp.transpose(jnp.concatenate(lefts, axis=1))
        right_col[slot] = jnp.concatenate(rights, axis=1)

    for i in range(i_dev):
        load_coef(i).wait()
    if "turn" not in SKIP:
        each(slots, order_row)
        each(slots, order_col)

    for i in range(i_dev):
        load_inter(i).wait()

    def prepare(index):
        scratch = more_scr.at[lax.rem(index, 2)]
        spread(inter[lax.div(index, j_dev), lax.rem(index, j_dev)], scratch)
        for n in range(2 * PARTNERS):
            packed = packed_of(scratch, n)
            flats[index, n] = packed.astype(BF16)
            squares[index, n] = split_twice(packed)

    if "coup" not in SKIP:
        twice(PREPARED, prepare)

    def pass_on(step):
        other = other_row(step)
        arrived(relay.at[other], recv_relay_sem.at[other])

        @pl.when(other != col)
        def _():
            to_col(other).start()

        @pl.when(other == col)
        def _():
            pltpu.make_async_copy(relay.at[other], col_one.at[col], recv_col_sem.at[col]).start()

    each(rows, pass_on)

    each(cols, lambda source: arrived(row_one.at[source], recv_row_sem.at[source]))

    def wanted(owner, slot):
        orbital = owner * i_dev + lax.div(slot, DOMAIN)
        atom = orbital_atoms[lax.rem(slot, DOMAIN), orbital] - owner * row_atoms
        atom = jnp.clip(atom, 0, row_atoms - 1)
        return lax.div(atom, per_dev), lax.rem(atom, per_dev)

    def pick_row(slot):
        source, place = wanted(row, slot)
        row_all[col, slot] = row_one[source, place]

    each(slots, pick_row)
    lines = jnp.zeros((16, HALF), F32)
    for slot in range(slots):
        source, place = wanted(row, slot)
        tile = row_one[source, per_dev].astype(F32)
        line = tile[0:1]
        for a in range(1, per_dev):
            line = jnp.where(place == a, tile[a : a + 1], line)
        lines = jnp.where(tile_row == slot, line, lines)
    lines_row[...] = lines

    def send_lines(other):
        return remote(lines_row, lines_col, send_lines_sem.at[other], recv_lines_sem.at[0], other, col)

    @pl.when(row == col)
    def _():
        each(rows - 1, lambda step: send_lines(other_row(step)).start())
        pltpu.make_async_copy(lines_row, lines_col, recv_lines_sem.at[0]).start()

    def part_of(ref, part):
        return ref.at[pl.ds(part * (slots // PARTS), slots // PARTS)]

    def gather_row(part, other):
        held = part_of(row_all.at[col], part)
        return remote(
            held, held, gather_row_sem.at[part, other], gathered_row_sem.at[part, col], row, other
        )

    def share_row(part, source):
        held = part_of(row_all.at[source], part)
        return remote(
            held, held, share_sem.at[part, source], gathered_row_sem.at[part, source], row, sibling
        )

    def row_arrived(part, source):
        arrived(part_of(row_all.at[source], part), gathered_row_sem.at[part, source])

    def peer(step):
        return lax.rem(col + 2 * (step + 1), cols)

    for part in range(PARTS):
        each(cols // 2 - 1, lambda step: gather_row(part, peer(step)).start())
        gather_row(part, sibling).start()

    if "coup" not in SKIP:
        each(i_dev * j_dev - PREPARED, lambda index: prepare(index + PREPARED))

    for place in range(4):
        arrived(halo.at[place], recv_halo_sem.at[place])

    def sources(place, block, first_row, first_col):
        def step(a):
            spread(block[a], spread_scr)
            for b in range(j_dev):
                packed = packed_of(spread_scr, b)
                doubled = twice_on_diagonal(packed, rows_scr.at[b])
                if first_row is not None:
                    source_row[first_row + a, b] = doubled
                if first_col is not None:
                    source_col[first_col + b, a] = doubled
                if first_row is not None and first_col is not None:
                    current[a * j_dev + b] = packed

        each(i_dev, step)

    if "coup" not in SKIP:
        sources(0, amplitudes, i_dev, j_dev)
        sources(0, halo.at[0], 0, None)
        sources(0, halo.at[1], 2 * i_dev, None)
        sources(0, halo.at[2], None, 0)
        sources(0, halo.at[3], None, 2 * j_dev)

    def couple(index):
        i, j = lax.div(index, j_dev), lax.rem(index, j_dev)
        halves = []
        for n in range(2 * PARTNERS):
            if n < PARTNERS:
                orbital = row * i_dev + i
                near = jnp.clip(fock_partner[n, orbital] - (row - 1) * i_dev, 0, 3 * i_dev - 1)
                partner = source_row[near, j]
                weight = fock_value[n, orbital]
            else:
                orbital = col * j_dev + j
                near = jnp.clip(
                    fock_partner[n - PARTNERS, orbital] - (col - 1) * j_dev, 0, 3 * j_dev - 1
                )
                partner = source_col[near, i]
                weight = fock_value[n - PARTNERS, orbital]
            half = jnp.dot(flats[index, n], partner, preferred_element_type=F32)
            halves.append((half * weight).astype(BF16))
        coupled[index] = lax.dot_general(
            jnp.concatenate(halves, axis=1),
            jnp.concatenate([squares[index, n] for n in range(2 * PARTNERS)], axis=1),
            (((1,), (1,)), ((), ())),
            preferred_element_type=F32,
        )

    if "coup" not in SKIP:
        twice(EARLY_PAIRS, couple)

    each(cols, lambda source: arrived(col_one.at[source], recv_col_sem.at[source]))

    def pick_col(slot):
        source, place = wanted(col, slot)
        col_pick[slot] = col_one[source, place]

    each(slots, pick_col)

    def gather_col(part, other):
        return remote(
            part_of(col_pick, part),
            part_of(col_all.at[row], part),
            gather_col_sem.at[part, other],
            gathered_col_sem.at[part, row],
            other,
            col,
        )

    def keep_col(part):
        return pltpu.make_async_copy(
            part_of(col_pick, part), part_of(col_all.at[row], part), gathered_col_sem.at[part, row]
        )

    def col_arrived(part, source):
        arrived(part_of(col_all.at[source], part), gathered_col_sem.at[part, source])

    for part in range(PARTS):
        each(rows - 1, lambda step: gather_col(part, other_row(step)).start())
        keep_col(part).start()

    if "coup" not in SKIP:
        twice(i_dev * j_dev - EARLY_PAIRS, lambda index: couple(index + EARLY_PAIRS))

    pick_from = lax.broadcasted_iota(jnp.int32, (LANES, LANES), 0)
    pick_to = lax.broadcasted_iota(jnp.int32, (LANES, LANES), 1)
    from_half, from_place = pick_from // NPNO, pick_from % NPNO
    ordered = from_half * NPNO + 2 * (from_place % (NPNO // 2)) + from_place // (NPNO // 2)
    order = jnp.where(ordered == pick_to, 1.0, 0.0).astype(BF16)
    at_row = 2 * lax.broadcasted_iota(jnp.int32, (CHUNKS, LANES), 0)
    at_lane = lax.broadcasted_iota(jnp.int32, (CHUNKS, LANES), 1)
    low = at_lane < NPNO
    level_a = at_row + jnp.where(low, 0, 1)
    level_b = jnp.where(low, at_lane, at_lane - NPNO)

    def local_part(i, j, along):
        index = i * j_dev + j
        sums = coupled[index]
        high = sums.astype(BF16)
        rest = (sums - high.astype(F32)).astype(BF16)
        coupling = jnp.dot(high, order, preferred_element_type=F32) + jnp.dot(
            rest, order, preferred_element_type=F32
        )
        at_b = jnp.broadcast_to(jnp.concatenate([along, along], axis=1), (CHUNKS, LANES))
        even = jnp.sum(jnp.where(at_lane == at_row, at_b, 0.0), axis=1, keepdims=True)
        odd = jnp.sum(jnp.where(at_lane == at_row + 1, at_b, 0.0), axis=1, keepdims=True)
        shift = at_b + jnp.where(low, even, odd)
        shift = shift - occupied[row * i_dev + i] - occupied[col * j_dev + j]
        coupled[index] = shift * current[index] - coupling

    def local_row(i):
        levels = energies[i]
        for j in range(j_dev):
            local_part(i, j, levels[j : j + 1])

    if "coup" not in SKIP:
        each(i_dev, local_row)

    def share(part):
        def step(number):
            source = peer(number)
            row_arrived(part, source)
            share_row(part, source).start()

        each(cols // 2 - 1, step)

    def from_sibling(part):
        each(cols // 2, lambda step: row_arrived(part, lax.rem(sibling + 2 * step, cols)))

    def build(held, lines, slot):
        packed = held[:, slot].reshape(PAO, HALF)
        last_line = lines[pl.ds(slot, 1), :]
        triangles = packed[:HALF].astype(F32)
        turned = jnp.transpose(triangles)
        cross = packed[HALF:].astype(F32)
        first = jnp.where(upper, turned, triangles)
        last = jnp.where(upper, triangles, jnp.where(lower, turned, last_line))
        metric[slot, :HALF, :HALF] = first.astype(BF16)
        metric[slot, :HALF, HALF:] = cross.astype(BF16)
        metric[slot, HALF:, :HALF] = jnp.transpose(cross).astype(BF16)
        metric[slot, HALF:, HALF:] = last.astype(BF16)

    def contract(part, left, right, total):
        def step(i):
            pieces = []
            for s in range(DOMAIN):
                slot = DOMAIN * i + s
                mapped = jnp.dot(metric[slot], right[slot], preferred_element_type=F32)
                pieces.append(
                    jnp.dot(left[slot], mapped.astype(BF16), preferred_element_type=F32)
                )
            whole = pieces[0] + pieces[1] + pieces[2]
            total[i, 0] = whole[:, :LANES]
            total[i, 1] = whole[:, LANES:]

        for i in range(i_dev // PARTS):
            step(i + part * (i_dev // PARTS))

    def build_all(part, held, lines):
        def step(i):
            for s in range(DOMAIN):
                build(held, lines, DOMAIN * i + s)

        for i in range(i_dev // PARTS):
            step(i + part * (i_dev // PARTS))

    for part in range(PARTS):
        share(part)
    for part in range(PARTS):
        from_sibling(part)
        if "build" not in SKIP:
            build_all(part, row_all, lines_row)
        if "dots" not in SKIP:
            contract(part, left_row, right_row, total_row)
    arrived(lines_col, recv_lines_sem.at[0])
    for part in range(PARTS):
        each(rows, lambda source: col_arrived(part, source))
        if "build" not in SKIP:
            build_all(part, col_all, lines_col)
        if "dots" not in SKIP:
            contract(part, left_col, right_col, total_col)

    def square_of(total, outer, inner):
        window = total.at[outer, inner // 2]
        even = window[pl.ds(NPNO * inner, CHUNKS, stride=2), :]
        odd = window[pl.ds(NPNO * inner + 1, CHUNKS, stride=2), :]
        if inner % 2 == 0:
            return jnp.where(low, even, swap_halves(odd))
        return jnp.where(low, swap_halves(even), odd)

    def store_out(i):
        return pltpu.make_async_copy(out_ref.at[i], out_hbm.at[i], out_sem.at[i])

    level = jnp.maximum(level_a, level_b)
    for i in range(i_dev):
        for j in range(j_dev):
            both = square_of(total_row, i, j) + square_of(total_col, j, i)
            result = both * (2 * DOMAIN * AUX) ** (-0.5) + coupled[i * j_dev + j]
            result = jnp.where(level < kept[i, j], result, 0.0)
            spread_scr[pl.ds(j, CHUNKS, stride=SUB), :] = result
        for k in range(CHUNKS):
            out_ref[i, :, LANES * k : LANES * k + LANES] = spread_scr[SUB * k : SUB * k + j_dev, :]
        store_out(i).start()

    def finish(step):
        to_plane(other_row(step)).wait_send()
        to_row(other_col(step)).wait_send()
        for part in range(PARTS):
            gather_col(part, other_row(step)).wait_send()
        to_col(other_col(step)).wait_send()

    each(rows - 1, finish)
    for i in range(i_dev):
        store_out(i).wait()
    for place in range(4):
        to_halo(place).wait_send()
    for part in range(PARTS):
        gather_row(part, sibling).wait_send()

    def finish_row(step):
        for part in range(PARTS):
            gather_row(part, peer(step)).wait_send()
            share_row(part, peer(step)).wait_send()

    each(cols // 2 - 1, finish_row)

    @pl.when(row == col)
    def _():
        each(rows - 1, lambda step: send_lines(other_row(step)).wait_send())


def on_device(
    fitting,
    coefficients,
    amplitudes,
    intersections,
    virtual_energy,
    occupied_energy,
    kept_count,
    orbital_atoms,
    fock_partner,
    fock_value,
):
    rows = lax.axis_size("row")
    cols = lax.axis_size("col")
    i_dev, j_dev = coefficients.shape[:2]
    per_dev = fitting.shape[0]
    slots = i_dev * DOMAIN
    pairs = i_dev * j_dev

    def body(*refs):
        residual_kernel(rows, cols, i_dev, j_dev, per_dev, *refs)

    dma = pltpu.SemaphoreType.DMA
    slices = (per_dev + 1, 16, HALF)
    hbm = pl.BlockSpec(memory_space=pl.ANY)
    return pl.pallas_call(
        body,
        out_shape=jax.ShapeDtypeStruct(amplitudes.shape, F32),
        in_specs=[hbm] * 10,
        out_specs=hbm,
        scratch_shapes=[
            pltpu.SMEM(orbital_atoms.shape[::-1], jnp.int32),
            pltpu.SMEM(fock_partner.shape[::-1], jnp.int32),
            pltpu.SMEM(fock_value.shape[::-1], F32),
            pltpu.SMEM(occupied_energy.shape, F32),
            pltpu.SMEM(kept_count.shape, jnp.int32),
            pltpu.VMEM(fitting.shape, BF16),
            pltpu.VMEM(amplitudes.shape, BF16),
            pltpu.VMEM(virtual_energy.shape, F32),
            pltpu.VMEM(amplitudes.shape, F32),
            pltpu.VMEM(coefficients.shape, BF16),
            pltpu.VMEM(intersections.shape, BF16),
            pltpu.VMEM((slots, PAO, PAO), BF16),
            pltpu.VMEM((slots, PAO, PAO), BF16),
            pltpu.VMEM((slots, PAO, PAO), BF16),
            pltpu.VMEM((slots, PAO, PAO), BF16),
            pltpu.VMEM((i_dev, 2, PAO, LANES), F32),
            pltpu.VMEM((j_dev, 2, PAO, LANES), F32),
            pltpu.VMEM((slots, PAO, PAO), BF16),
            pltpu.VMEM((cols,) + slices, BF16),
            pltpu.VMEM((rows, per_dev, 16, HALF), BF16),
            pltpu.VMEM((cols,) + slices, BF16),
            pltpu.VMEM((cols, per_dev, 16, HALF), BF16),
            pltpu.VMEM((slots, 16, HALF), BF16),
            pltpu.VMEM((cols, slots, 16, HALF), BF16),
            pltpu.VMEM((rows, slots, 16, HALF), BF16),
            pltpu.VMEM((4,) + amplitudes.shape, BF16),
            pltpu.VMEM((3 * i_dev, j_dev, LANES, LANES), BF16),
            pltpu.VMEM((3 * j_dev, i_dev, LANES, LANES), BF16),
            pltpu.VMEM((pairs, CHUNKS, LANES), F32),
            pltpu.VMEM((pairs, CHUNKS, LANES), F32),
            pltpu.VMEM((SUB * CHUNKS, LANES), F32),
            pltpu.VMEM((j_dev, NPNO, LANES), F32),
            pltpu.VMEM((16, HALF), F32),
            pltpu.VMEM((16, HALF), F32),
            pltpu.VMEM((pairs, 2 * PARTNERS, CHUNKS, LANES), BF16),
            pltpu.VMEM((pairs, 2 * PARTNERS, LANES, LANES), BF16),
            pltpu.VMEM((2, SUB * CHUNKS, LANES), F32),
            dma((i_dev,)),
            dma((i_dev,)),
        ]
        + [dma((rows,))] * 6
        + [dma((PARTS, rows))] * 5
        + [dma((4,))] * 2
        + [dma((8,)), dma((i_dev,)), dma((rows,)), dma((1,))],
        compiler_params=pltpu.CompilerParams(
            collective_id=0, has_side_effects=True, vmem_limit_bytes=62 * 1024 * 1024
        ),
        name="residual",
    )(
        orbital_atoms.T,
        fock_partner.T,
        fock_value.T,
        occupied_energy,
        kept_count,
        fitting,
        amplitudes,
        virtual_energy,
        coefficients,
        intersections,
    )


def solution(mesh):
    placed = (
        P(("row", "col"), None, None),
        P("row", "col", None, None, None),
        P("row", "col", None),
        P("row", "col", None, None),
        P("row", "col", None),
        P(),
        P("row", "col"),
        P(),
        P(),
        P(),
    )
    return jax.shard_map(
        on_device, mesh=mesh, in_specs=placed, out_specs=P("row", "col", None), check_vma=False
    )
```
